128 devices in a mesh: wide: 16 (over z, y_lo, core), narrow: 8 (over x, y_hi).
Axes of the slice: x: 4, y: 4 (y_hi: 2, y_lo: 2; y = y_hi * 2 + y_lo), z: 4, core: 2. Of those that a mesh axis runs over, the one named last changes fastest.
Arguments:
- tridiag_vectors: float32 [128, 131072], P(('wide', 'narrow')), may hold values from -6 to 6
- reflectors: float32 [2, 131072, 256], P(None, 'wide'), may hold values from -0.015625 to 0.015625
- triangles: float32 [2, 256, 256], replicated, as said below
- lower_blocks: float32 [6, 1536, 1536], P(None, 'wide'), may hold values from -0.109375 to 0.109375
- diag_inverses: float32 [4, 1536, 1536], P(None, None, 'wide'), as said below
Outputs:
- transformed: float32 [128, 131072], P('narrow', 'wide')
- solved: float32 [128, 4, 1536], P('narrow', None, 'wide')
The draws below stay inside these ranges and needn't reach their ends.
Inputs may be any that keep to these rules, and one draw needn't show every extreme that they name: `triangles`: zero below the diagonal, positive on it. `diag_inverses`: zero above the diagonal, positive on it.
All inputs are finite; a program needn't handle non-finite values.
Results may differ from the reference program's by a relative error of at most 0.00019.
Values sent between devices are 32-bit elements; how exact they have to be, the bound alone decides.
No kernel may reach another device: no remote copies, remote signals or barrier semaphores. Data moves between devices by JAX's collectives and lax.ppermute only.
A program may use at most 128 MiB of HBM per device.

```python
import math
import jax
import jax.numpy as jnp
from jax import lax

N = 131072
K = 128
NB = 256
PANELS = 4
PANEL = 1536
BLOCKS = 6


def draw_triangles(key, part):
    key_diag, key_upper = jax.random.split(jax.random.fold_in(key, 11))
    factor = math.sqrt(N / NB)
    diagon = jnp.exp(jax.random.uniform(key_diag, (2, NB), jnp.float32, math.log(0.5), math.log(2.0)))
    upper = jax.random.truncated_normal(key_upper, -4.0, 4.0, (2, NB, NB), jnp.float32) / math.sqrt(NB)
    strict = jnp.triu(jnp.ones((NB, NB), jnp.float32), 1)
    return factor * (upper * strict + diagon[:, :, None] * jnp.eye(NB, dtype=jnp.float32))


def draw_diag_inverses(key, part):
    key_diag, key_lower = jax.random.split(jax.random.fold_in(key, 23))
    diagon = jnp.exp(jax.random.uniform(key_diag, (PANELS, PANEL), jnp.float32, math.log(0.5), math.log(2.0)))
    lower = 0.5 * jax.random.truncated_normal(key_lower, -4.0, 4.0, (PANELS, PANEL, PANEL), jnp.float32) / math.sqrt(PANEL)
    strict = jnp.tril(jnp.ones((PANEL, PANEL), jnp.float32), -1)
    return lower * strict + diagon[:, :, None] * jnp.eye(PANEL, dtype=jnp.float32)


def shard_levels(key, shape, pieces, smallest, high):
    loudness = 1.0
    for dim, shards_of in pieces:
        draws = jax.random.uniform(jax.random.fold_in(jax.random.fold_in(key, 6), dim), (shards_of,), jnp.float32, smallest / len(pieces), high / len(pieces))
        loudness = loudness * jnp.repeat(jnp.exp(draws), shape[dim] // shards_of).reshape((-1,) + (1,) * (len(shape) - 1 - dim))
    return loudness


def scatter_about(stream_key, dims, deviation, bound, shards=(), held_as=jnp.bfloat16):
    drawn = jax.random.normal(stream_key, dims, jnp.float32) * deviation
    if len(shards) > 0:
        drawn = shard_levels(stream_key, dims, shards, -0.22, 0.18) * drawn
    return jnp.clip(drawn, min=-bound, max=bound).astype(held_as)


def setup_inputs(seed: int = 0) -> dict:
    seeds = jax.random.split(jax.random.key(seed), 6)
    tridiag_vectors = scatter_about(seeds[0], (K, N), 1.0, 6.0, ((0, 128),), jnp.float32)
    reflectors = scatter_about(seeds[1], (2, N, NB), N ** -0.5, 0.015625, ((1, 16),), jnp.float32)
    triangles = draw_triangles(jax.random.fold_in(seeds[5], 71), 0)
    lower_blocks = scatter_about(seeds[3], (BLOCKS, PANEL, PANEL), (2 * PANEL) ** -0.5, 0.109375, ((1, 16),), jnp.float32)
    diag_inverses = draw_diag_inverses(jax.random.fold_in(seeds[5], 71), 0)
    return dict(tridiag_vectors=tridiag_vectors, reflectors=reflectors, triangles=triangles, lower_blocks=lower_blocks, diag_inverses=diag_inverses)


HIGHEST = lax.Precision.HIGHEST


def reference(tridiag_vectors, reflectors, triangles, lower_blocks, diag_inverses):
    current = tridiag_vectors
    for which in (1, 0):
        products = jnp.dot(current, reflectors[which], precision=HIGHEST)
        coeffs = jnp.dot(products, triangles[which].T, precision=HIGHEST)
        current = current - jnp.dot(coeffs, reflectors[which].T, precision=HIGHEST)
    corner = current[:, N - PANELS * PANEL:].reshape(K, PANELS, PANEL)
    results = [None] * PANELS
    for source in reversed(range(PANELS)):
        remain = corner[:, source, :]
        for higher in range(source + 1, PANELS):
            index_block = higher * (higher - 1) // 2 + source
            remain = remain - jnp.dot(results[higher], lower_blocks[index_block], precision=HIGHEST)
        results[source] = jnp.dot(remain, diag_inverses[source], precision=HIGHEST)
    return current, jnp.stack(results, axis=1)
```

```python
import jax
import jax.numpy as jnp
from jax import lax
from jax.sharding import PartitionSpec as P

HIGH = lax.Precision.HIGH


def dot(a, b):
    return jnp.dot(a, b, precision=HIGH)


def from_everyone(array, axis):
    devices = lax.axis_size(axis)
    return lax.all_to_all(
        jnp.broadcast_to(array[None], (devices, *array.shape)), axis, 0, 0, tiled=True
    )


def swapped(array):
    size = lax.axis_size("wide")
    return lax.ppermute(array, "wide", [(i, i ^ 1) for i in range(size)])


def summed_over_chips(array):
    size = lax.axis_size("wide")
    array = array + lax.ppermute(array, "wide", [(i, i ^ 2) for i in range(size)])
    far = lax.ppermute(array, "wide", [(i, (i + 8) % size) for i in range(size)])
    up = lax.ppermute(array, "wide", [(i, (i + 4) % size) for i in range(size)])
    down = lax.ppermute(array, "wide", [(i, (i + 12) % size) for i in range(size)])
    return (array + far) + (up + down)


def from_last_chip(array, is_last):
    size = lax.axis_size("wide")
    array = jnp.where(is_last, array, 0.0)
    last = size - 2
    total = array
    for back in (8, 4, 12):
        pairs = [(last + c, (last + c + back) % size) for c in range(2)]
        total = total + lax.ppermute(array, "wide", pairs)
    pairs = [(i, i ^ 2) for i in range(size) if i & 2]
    return total + lax.ppermute(total, "wide", pairs)


def solve_chain(tail, lower_blocks, diag_inverses):
    count = tail.shape[0]
    panels, rows, share = diag_inverses.shape
    half = rows // 2
    me = lax.axis_index("wide")
    core = me % 2
    is_last = me >= lax.axis_size("wide") - 2
    mine, other = core * half, (1 - core) * half
    turned = jnp.swapaxes(diag_inverses, 1, 2)
    d_keep = lax.dynamic_slice_in_dim(turned, mine, half, 2)
    d_send = lax.dynamic_slice_in_dim(turned, other, half, 2)
    d_pair = jnp.concatenate([d_keep, swapped(d_send)], axis=1)
    l_keep = lax.dynamic_slice_in_dim(lower_blocks, mine, half, 2)
    l_send = lax.dynamic_slice_in_dim(lower_blocks, other, half, 2)
    l_pair = jnp.concatenate([l_keep, swapped(l_send)], axis=1)
    tail = tail.reshape(count, panels, 2, half)
    corner = jnp.where(
        me == lax.axis_size("wide") - 1, tail[:, :, 1, :], swapped(tail[:, :, 0, :])
    )
    remain = from_last_chip(corner[:, panels - 1, :], is_last)
    pending = [jnp.where(is_last, corner[:, p, :], 0.0) for p in range(panels - 1)]
    results = [None] * panels
    for source in reversed(range(panels)):
        part = lax.dot_general(
            remain, d_pair[source], (((1,), (1,)), ((), ())), precision=HIGH
        )
        back = jnp.concatenate([part[:, share:], part[:, :share]], axis=1)
        pair = part + swapped(back)
        results[source] = pair[:, :share]
        offset = source * (source - 1) // 2
        for target in range(source):
            pending[target] = pending[target] - dot(pair, l_pair[offset + target])
        if source > 0:
            remain = summed_over_chips(pending[source - 1])
    return jnp.stack(results, axis=1)


def body(tridiag_vectors, reflectors, triangles, lower_blocks, diag_inverses):
    wide_size = lax.axis_size("wide")
    narrow_size = lax.axis_size("narrow")
    current = lax.all_to_all(
        lax.all_to_all(tridiag_vectors, "wide", split_axis=1, concat_axis=0, tiled=True),
        "narrow",
        split_axis=0,
        concat_axis=0,
        tiled=True,
    )
    per_device = tridiag_vectors.shape[0]
    length = current.shape[1]
    current = current.reshape(narrow_size, wide_size // narrow_size, per_device, length)
    current = current.transpose(1, 0, 2, 3).reshape(-1, length)
    for which in (1, 0):
        parts = from_everyone(dot(current, reflectors[which]), "wide")
        coeffs = dot(jnp.sum(parts, axis=0), triangles[which].T)
        current = current - dot(coeffs, reflectors[which].T)
    panels, panel_rows, _ = diag_inverses.shape
    tail = current[:, length - panels * panel_rows :]
    solved = solve_chain(tail, lower_blocks, diag_inverses)
    return (current, solved)


def solution(mesh):
    placed = (
        P(("wide", "narrow"), None),
        P(None, "wide", None),
        P(),
        P(None, "wide", None),
        P(None, None, "wide"),
    )
    return jax.shard_map(
        body,
        mesh=mesh,
        in_specs=placed,
        out_specs=(P("narrow", "wide"), P("narrow", None, "wide")),
        check_vma=False,
    )
```

```python
import functools

import jax
import jax.numpy as jnp
from jax import lax
from jax.experimental import pallas as pl
from jax.experimental.pallas import tpu as pltpu
from jax.sharding import PartitionSpec as P

HIGH = lax.Precision.HIGH
NN = (((1,), (0,)), ((), ()))
NT = (((1,), (1,)), ((), ()))


def dot(a, b):
    return jnp.dot(a, b, precision=HIGH)


def split(x):
    high = x.astype(jnp.bfloat16)
    return high, (x - high.astype(jnp.float32)).astype(jnp.bfloat16)


def dot_split(a, b, dims):
    rows = a[0].shape[0]
    both = jnp.concatenate(a, axis=0)
    with_high = lax.dot_general(both, b[0], dims, preferred_element_type=jnp.float32)
    with_low = lax.dot_general(a[0], b[1], dims, preferred_element_type=jnp.float32)
    return with_high[:rows] + (with_high[rows:] + with_low)


def in_vmem(count):
    return [pl.BlockSpec(memory_space=pltpu.VMEM)] * count


BIG = pltpu.CompilerParams(vmem_limit_bytes=50 << 20)


def streamed(v_ref, held, sems, first, count, use):
    unit = held.shape[2]
    slots = held.shape[0]

    def fetch(i):
        where = pl.ds((first + i) * unit, unit)
        return pltpu.make_async_copy(
            v_ref.at[:, where, :], held.at[i % slots], sems.at[i % slots]
        )

    for i in range(min(slots, count)):
        fetch(i).start()
    for i in range(count):
        fetch(i).wait()
        use(i, held.at[i % slots])
        if i + slots < count:
            fetch(i + slots).start()


def products_kernel(z_ref, v_ref, flat_ref, p1_ref, p0_ref, held, sems):
    unit = held.shape[2]
    _, per, subs, lanes = z_ref.shape
    sums = [jnp.zeros(p1_ref.shape, jnp.float32) for _ in range(2)]

    def use(i, v_ref):
        columns = []
        for s in range(i * unit // lanes, (i + 1) * unit // lanes):
            rows = [z_ref[:, c, s, :] for c in range(per)]
            columns.append(jnp.concatenate(rows, axis=0))
        z = jnp.concatenate(columns, axis=1)
        flat_ref[:, i * unit : (i + 1) * unit] = z
        z = split(z)
        for which in range(2):
            sums[which] = sums[which] + dot_split(z, split(v_ref[which]), NN)

    streamed(v_ref, held, sems, 0, subs * lanes // unit, use)
    p1_ref[...] = sums[1]
    p0_ref[...] = sums[0]


def products_of(received, reflectors):
    parts, per, subs, lanes = received.shape
    rows = parts * per
    length = subs * lanes
    block = reflectors.shape[2]
    sums = jax.ShapeDtypeStruct((rows, block), jnp.float32)
    return pl.pallas_call(
        products_kernel,
        out_shape=[jax.ShapeDtypeStruct((rows, length), jnp.float32), sums, sums],
        in_specs=in_vmem(1) + [pl.BlockSpec(memory_space=pl.ANY)],
        out_specs=in_vmem(3),
        scratch_shapes=held_pieces(block, 512, 6),
        compiler_params=BIG,
        cost_estimate=update_cost(rows, length, block),
    )(received, reflectors)


def pieces_of(z_ref, coeffs_ref, v_ref, held, sems, first, count, write):
    unit = held.shape[2]
    block = v_ref.shape[2]
    coeffs = [
        split(coeffs_ref[:, slot * block : (slot + 1) * block]) for slot in range(2)
    ]

    def use(i, piece_ref):
        total = z_ref[:, (first + i) * unit : (first + i + 1) * unit]
        for slot, which in enumerate((1, 0)):
            total = total - dot_split(coeffs[slot], split(piece_ref[which]), NT)
        write(i, total)

    streamed(v_ref, held, sems, first, count, use)


def corner_kernel(first, z_ref, coeffs_ref, v_ref, o_ref, held, sems):
    unit = held.shape[2]
    _, panels, _, half = o_ref.shape
    each = half // unit

    def write(i, total):
        p, h, k = i // (2 * each), (i // each) % 2, i % each
        o_ref[h, p, :, k * unit : (k + 1) * unit] = total

    count = 2 * panels * each
    pieces_of(z_ref, coeffs_ref, v_ref, held, sems, first, count, write)


def final_kernel(z_ref, coeffs_ref, v_ref, rest_ref, last_ref, o_ref, held, sems):
    unit = held.shape[2]
    _, others, _, half = rest_ref.shape
    start = o_ref.shape[1] - 2 * half * (others + 1)

    def write(i, total):
        o_ref[:, i * unit : (i + 1) * unit] = total

    pieces_of(z_ref, coeffs_ref, v_ref, held, sems, 0, start // unit, write)
    for p in range(others + 1):
        for h in range(2):
            piece = rest_ref[h, p] if p < others else last_ref[h, 0]
            at = start + (2 * p + h) * half
            o_ref[:, at : at + half] = piece


UNIT = 256


def held_pieces(block, unit, slots):
    return [
        pltpu.VMEM((slots, 2, unit, block), jnp.float32),
        pltpu.SemaphoreType.DMA((slots,)),
    ]


def update_cost(rows, columns, block):
    return pl.CostEstimate(
        flops=12 * rows * columns * block,
        bytes_accessed=8 * columns * block + 8 * rows * columns,
        transcendentals=0,
    )


def corner_of(flat, coeffs, reflectors, first, panels, half):
    rows = flat.shape[0]
    block = reflectors.shape[2]
    return pl.pallas_call(
        functools.partial(corner_kernel, first // UNIT),
        out_shape=jax.ShapeDtypeStruct((2, panels, rows, half), jnp.float32),
        in_specs=in_vmem(2) + [pl.BlockSpec(memory_space=pl.ANY)],
        out_specs=in_vmem(1)[0],
        scratch_shapes=held_pieces(block, UNIT, 6),
        compiler_params=BIG,
        cost_estimate=update_cost(rows, 2 * panels * half, block),
    )(flat, coeffs, reflectors)


def transformed_of(flat, coeffs, reflectors, rest, last):
    rows, columns = flat.shape
    block = reflectors.shape[2]
    start = columns - (rest.size + last.size) // rows
    return pl.pallas_call(
        final_kernel,
        out_shape=jax.ShapeDtypeStruct((rows, columns), jnp.float32),
        in_specs=in_vmem(2) + [pl.BlockSpec(memory_space=pl.ANY)] + in_vmem(2),
        out_specs=in_vmem(1)[0],
        scratch_shapes=held_pieces(block, UNIT, 6),
        compiler_params=BIG,
        cost_estimate=update_cost(rows, start, block),
    )(flat, coeffs, reflectors, rest, last)


def swapped(array):
    size = lax.axis_size("wide")
    return lax.ppermute(array, "wide", [(i, i ^ 1) for i in range(size)])


def from_chips(array):
    size = lax.axis_size("wide")
    array = array + lax.ppermute(array, "wide", [(i, i ^ 2) for i in range(size)])
    others = [
        lax.ppermute(array, "wide", [(i, (i + by) % size) for i in range(size)])
        for by in (8, 4, 12)
    ]
    return array, *others


def summed_over_wide(array):
    own, far, up, down = from_chips(array + swapped(array))
    return (own + far) + (up + down)


def from_last_chip(array, is_last, beside):
    size = lax.axis_size("wide")
    array = jnp.where(is_last, array, 0.0)
    last = size - 2
    total = array
    for back in (8, 4, 12):
        pairs = [(last + c, (last + c + back) % size) for c in range(2)]
        total = total + lax.ppermute(array, "wide", pairs)
    pairs = [(i, i ^ 2) for i in range(size) if i & 2]
    total, beside = lax.optimization_barrier((total, beside))
    return total + lax.ppermute(total, "wide", pairs), beside


def half_pairs(arrays, others, half):
    mine = (lax.axis_index("wide") % 2) * half
    return [
        jnp.concatenate(
            [lax.dynamic_slice_in_dim(x, mine, half, 2) for x in (array, other)], axis=1
        )
        for array, other in zip(arrays, others)
    ]


def own_half(halves):
    is_owner = lax.axis_index("wide") == lax.axis_size("wide") - 1
    return jnp.where(is_owner, halves[1], swapped(halves[0]))


def solve_chain(remain, rest, d_pair, l_pair, is_last):
    panels, pair_cols, half = d_pair.shape
    share = pair_cols // 2
    rest = own_half(rest)
    pending = [jnp.where(is_last, rest[p], 0.0) for p in range(panels - 1)]
    results = [None] * panels
    for source in reversed(range(panels)):
        part = lax.dot_general(remain, d_pair[source], NT, precision=HIGH)
        back = jnp.concatenate([part[:, share:], part[:, :share]], axis=1)
        pair = part + swapped(back)
        results[source] = pair[:, :share]
        offset = source * (source - 1) // 2
        for target in range(source):
            pending[target] = pending[target] - dot(pair, l_pair[offset + target])
        if source > 0:
            own, far, up, down = from_chips(pending[source - 1])
            remain = (own + far) + (up + down)
    return jnp.stack(results, axis=1)


def gram_of(reflectors, lo, hi):
    return lax.dot_general(
        reflectors[1, lo:hi],
        reflectors[0, lo:hi],
        (((0,), (0,)), ((), ())),
        precision=HIGH,
    )


def body(tridiag_vectors, reflectors, triangles, lower_blocks, diag_inverses):
    wide_size = lax.axis_size("wide")
    narrow_size = lax.axis_size("narrow")
    _, length, block = reflectors.shape
    panels, panel_rows, _ = diag_inverses.shape
    half = panel_rows // 2
    subs = length // 128
    weights = (jnp.swapaxes(diag_inverses, 1, 2), lower_blocks)
    traded = [swapped(array) for array in weights]

    received = tridiag_vectors.reshape(wide_size, subs, 128)
    received = lax.all_to_all(received, "wide", 0, 0, tiled=True)
    gram = gram_of(reflectors, 0, length // 2)
    received, gram = lax.optimization_barrier((received, gram))
    received, later = lax.optimization_barrier((received, reflectors))
    received = lax.all_to_all(received, "narrow", 0, 0, tiled=True)
    gram = gram + gram_of(later, length // 2, length)
    received, gram, weights = lax.optimization_barrier((received, gram, weights))
    per = wide_size // narrow_size
    received = received.reshape(narrow_size, per, subs, 128)
    flat, first, second = products_of(received, reflectors)
    coeffs1 = dot(summed_over_wide(first), triangles[1].T)
    second = second - dot(coeffs1, gram)
    second = summed_over_wide(second)
    d_pair, l_pair = half_pairs(weights, traded, half)
    second, d_pair, l_pair = lax.optimization_barrier((second, d_pair, l_pair))
    coeffs0 = dot(second, triangles[0].T)
    coeffs = jnp.concatenate([coeffs1, coeffs0], axis=1)

    is_last = lax.axis_index("wide") >= wide_size - 2
    start = length - panels * panel_rows
    last = corner_of(flat, coeffs, reflectors, length - panel_rows, 1, half)
    corner = own_half(last)[0]
    corner, late = lax.optimization_barrier((corner, coeffs))
    rest = corner_of(flat, late, reflectors, start, panels - 1, half)
    remain, rest = from_last_chip(corner, is_last, rest)
    remain, late = lax.optimization_barrier((remain, late))
    transformed = transformed_of(flat, late, reflectors, rest, last)
    solved = solve_chain(remain, rest, d_pair, l_pair, is_last)
    return (transformed, solved)


def solution(mesh):
    placed = (
        P(("wide", "narrow"), None),
        P(None, "wide", None),
        P(),
        P(None, "wide", None),
        P(None, None, "wide"),
    )
    return jax.shard_map(
        body,
        mesh=mesh,
        in_specs=placed,
        out_specs=(P("narrow", "wide"), P("narrow", None, "wide")),
        check_vma=False,
    )
```

```python
import functools

import jax
import jax.numpy as jnp
from jax import lax
from jax.experimental import pallas as pl
from jax.experimental.pallas import tpu as pltpu
from jax.sharding import PartitionSpec as P

HIGH = lax.Precision.HIGH
NN = (((1,), (0,)), ((), ()))
NT = (((1,), (1,)), ((), ()))


def dot(a, b):
    return jnp.dot(a, b, precision=HIGH)


def dot_nt(a, b):
    return lax.dot_general(a, b, NT, precision=HIGH)


def split(x):
    high = x.astype(jnp.bfloat16)
    return high, (x - high.astype(jnp.float32)).astype(jnp.bfloat16)


def dot_split(a, b, dims):
    rows = a[0].shape[0]
    both = jnp.concatenate(a, axis=0)
    with_high = lax.dot_general(both, b[0], dims, preferred_element_type=jnp.float32)
    with_low = lax.dot_general(a[0], b[1], dims, preferred_element_type=jnp.float32)
    return with_high[:rows] + (with_high[rows:] + with_low)


def in_vmem(count):
    return [pl.BlockSpec(memory_space=pltpu.VMEM)] * count


BIG = pltpu.CompilerParams(vmem_limit_bytes=50 << 20)


def held_pieces(block, which, unit, slots):
    return [
        pltpu.VMEM((slots, which, unit, block), jnp.float32),
        pltpu.SemaphoreType.DMA((slots, which)),
    ]


def dot_cost(rows, inner, outer):
    return pl.CostEstimate(
        flops=6 * rows * inner * outer,
        bytes_accessed=4 * (inner * outer + rows * inner + rows * outer),
        transcendentals=0,
    )


def pair_kernel(core_ref, own_ref, other_ref, o_ref, held, sems):
    _, pair, half = o_ref.shape
    share = pair // 2
    core = core_ref[0]
    where = pl.ds(pl.multiple_of(core * half, 128), half)
    moves = []
    for slot, (source, at) in enumerate(((own_ref, core), (other_ref, 1 - core))):
        to = o_ref.at[:, pl.ds(pl.multiple_of(at * share, 8), share), :]
        step = held.at[slot]
        moves.append(
            (
                pltpu.make_async_copy(source.at[:, :, where], step, sems.at[slot]),
                pltpu.make_async_copy(step, to, sems.at[2 + slot]),
            )
        )
    for fetch, _ in moves:
        fetch.start()
    for fetch, store in moves:
        fetch.wait()
        store.start()
    for _, store in moves:
        store.wait()


def half_pair(own, other, half):
    core = (lax.axis_index("wide") % 2)[None]
    count, share, _ = own.shape
    out = jax.ShapeDtypeStruct((count, 2 * share, half), own.dtype)
    return pl.pallas_call(
        pair_kernel,
        out_shape=out,
        in_specs=[pl.BlockSpec(memory_space=pltpu.SMEM)]
        + [pl.BlockSpec(memory_space=pl.ANY)] * 2,
        out_specs=pl.BlockSpec(memory_space=pl.ANY),
        scratch_shapes=[
            pltpu.VMEM((2, count, share, half), own.dtype),
            pltpu.SemaphoreType.DMA((4,)),
        ],
        compiler_params=pltpu.CompilerParams(vmem_limit_bytes=60 << 20),
        cost_estimate=pl.CostEstimate(
            flops=0, bytes_accessed=out.size, transcendentals=0
        ),
    )(core, own, other)


def streamed(v_ref, held, sems, which, first, count, use):
    unit = held.shape[2]
    slots = held.shape[0]

    def fetches(i):
        where = pl.ds(first + i * unit, unit)
        slot = i % slots
        return [
            pltpu.make_async_copy(
                v_ref.at[w, where, :], held.at[slot, j], sems.at[slot, j]
            )
            for j, w in enumerate(which)
        ]

    def start(i):
        for copy in fetches(i):
            copy.start()

    for i in range(min(slots, count)):
        start(i)
    for i in range(count):
        for copy in fetches(i):
            copy.wait()
        use(i, held.at[i % slots])
        if i + slots < count:
            start(i + slots)


def products_kernel(z_ref, v_ref, flat_ref, p1_ref, p0_ref, held, sems):
    unit = held.shape[2]
    _, per, subs, lanes = z_ref.shape
    sums = [jnp.zeros(p1_ref.shape, jnp.float32) for _ in range(2)]

    def use(i, v_ref):
        columns = []
        for s in range(i * unit // lanes, (i + 1) * unit // lanes):
            rows = [z_ref[:, c, s, :] for c in range(per)]
            columns.append(jnp.concatenate(rows, axis=0))
        z = jnp.concatenate(columns, axis=1)
        flat_ref[:, i * unit : (i + 1) * unit] = z
        z = split(z)
        for which in range(2):
            sums[which] = sums[which] + dot_split(z, split(v_ref[which]), NN)

    streamed(v_ref, held, sems, (0, 1), 0, subs * lanes // unit, use)
    p1_ref[...] = sums[1]
    p0_ref[...] = sums[0]


def products_of(received, reflectors):
    parts, per, subs, lanes = received.shape
    rows = parts * per
    length = subs * lanes
    block = reflectors.shape[2]
    sums = jax.ShapeDtypeStruct((rows, block), jnp.float32)
    return pl.pallas_call(
        products_kernel,
        out_shape=[jax.ShapeDtypeStruct((rows, length), jnp.float32), sums, sums],
        in_specs=in_vmem(1) + [pl.BlockSpec(memory_space=pl.ANY)],
        out_specs=in_vmem(3),
        scratch_shapes=held_pieces(block, 2, 1024, 4),
        compiler_params=BIG,
        cost_estimate=dot_cost(rows, length, 2 * block),
    )(received, reflectors)


def pieces_of(z_ref, z_first, coeffs, v_ref, held, sems, which, first, count, write):
    unit = held.shape[2]
    coeffs = [split(ref[...]) for ref in coeffs]

    def use(i, piece_ref):
        at = z_first + i * unit
        total = z_ref[:, at : at + unit]
        for j, part in enumerate(coeffs):
            total = total - dot_split(part, split(piece_ref[j]), NT)
        write(i, total)

    streamed(v_ref, held, sems, which, first, count, use)


def update_kernel(z_first, first, which, z_ref, v_ref, *refs):
    *coeffs, o_ref, held, sems = refs
    unit = held.shape[2]
    if len(o_ref.shape) == 2:
        count = o_ref.shape[1] // unit

        def write(i, total):
            o_ref[:, i * unit : (i + 1) * unit] = total

    else:
        _, panels, _, half = o_ref.shape
        each = half // unit
        count = 2 * panels * each

        def write(i, total):
            p, h, k = i // (2 * each), (i // each) % 2, i % each
            o_ref[h, p, :, k * unit : (k + 1) * unit] = total

    pieces_of(z_ref, z_first, coeffs, v_ref, held, sems, which, first, count, write)


def updated(z, z_first, coeffs, reflectors, which, first, out, unit):
    block = reflectors.shape[2]
    rows = z.shape[0]
    columns = out[1] if len(out) == 2 else 2 * out[1] * out[3]
    return pl.pallas_call(
        functools.partial(update_kernel, z_first, first, which),
        out_shape=jax.ShapeDtypeStruct(out, jnp.float32),
        in_specs=in_vmem(1) + [pl.BlockSpec(memory_space=pl.ANY)] + in_vmem(len(which)),
        out_specs=in_vmem(1)[0],
        scratch_shapes=held_pieces(block, len(which), unit, 4),
        compiler_params=BIG,
        cost_estimate=dot_cost(rows, len(which) * block, columns),
    )(z, reflectors, *coeffs)


def joined_kernel(first_ref, *refs):
    *pieces, o_ref = refs
    at = first_ref.shape[1]
    o_ref[:, :at] = first_ref[...]
    for ref in pieces:
        half = ref.shape[3]
        for q in range(ref.shape[1]):
            for h in range(2):
                o_ref[:, at : at + half] = ref[h, q]
                at += half


def joined(first, pieces):
    rows = first.shape[0]
    size = first.size + sum(x.size for x in pieces)
    return pl.pallas_call(
        joined_kernel,
        out_shape=jax.ShapeDtypeStruct((rows, size // rows), jnp.float32),
        in_specs=in_vmem(1 + len(pieces)),
        out_specs=in_vmem(1)[0],
        cost_estimate=pl.CostEstimate(
            flops=0, bytes_accessed=8 * size, transcendentals=0
        ),
    )(first, *pieces)


def swapped(array):
    size = lax.axis_size("wide")
    return lax.ppermute(array, "wide", [(i, i ^ 1) for i in range(size)])


def from_chips(array, beside=()):
    size = lax.axis_size("wide")
    array = array + lax.ppermute(array, "wide", [(i, i ^ 2) for i in range(size)])
    array, beside = lax.optimization_barrier((array, beside))
    others = [
        lax.ppermute(array, "wide", [(i, (i + by) % size) for i in range(size)])
        for by in (4, 8, 12)
    ]
    return (array + others[0]) + (others[1] + others[2]), beside


def summed_over_wide(array, beside):
    return from_chips(array + swapped(array), beside)


def from_last_chip(array, is_last, beside):
    size = lax.axis_size("wide")
    array = jnp.where(is_last, array, 0.0)
    last = size - 2
    total = array
    for back in (12, 4, 8):
        pairs = [(last + c, (last + c + back) % size) for c in range(2)]
        total = total + lax.ppermute(array, "wide", pairs)
    pairs = [(i, i ^ 2) for i in range(size) if i & 2]
    total, beside = lax.optimization_barrier((total, beside))
    return total, total + lax.ppermute(total, "wide", pairs), beside


def own_half(halves):
    is_owner = lax.axis_index("wide") == lax.axis_size("wide") - 1
    return jnp.where(is_owner, halves[1], swapped(halves[0]))


def solve_chain(remain, rest, d_pair, l_pair, is_last, late, fillers):
    panels, pair_cols, _ = d_pair.shape
    share = pair_cols // 2
    pending = []
    for piece in rest:
        owned = own_half(piece)
        pending += [jnp.where(is_last, x, 0.0) for x in owned]
    first_core = lax.axis_index("wide") % 2 == 0
    results = [None] * panels
    for source in reversed(range(panels)):
        part = dot_nt(remain, d_pair[source])
        pair = part + swapped(part)
        results[source] = jnp.where(first_core, pair[:, :share], pair[:, share:])
        offset = source * (source - 1) // 2
        for target in reversed(range(source)):
            pending[target] = pending[target] - dot(pair, l_pair[offset + target])
        if source > 0:
            urgent, late = lax.optimization_barrier((pending[source - 1], late))
            late = fillers[panels - 1 - source](late)
            remain, late = from_chips(urgent, late)
    return late, jnp.stack(results, axis=1)


def gram_of(reflectors, lo, hi):
    return lax.dot_general(
        reflectors[1, lo:hi],
        reflectors[0, lo:hi],
        (((0,), (0,)), ((), ())),
        precision=HIGH,
    )


def body(tridiag_vectors, reflectors, triangles, lower_blocks, diag_inverses):
    wide_size = lax.axis_size("wide")
    narrow_size = lax.axis_size("narrow")
    _, length, block = reflectors.shape
    panels, panel_rows, _ = diag_inverses.shape
    half = panel_rows // 2
    subs = length // 128
    last = length - panel_rows
    is_owner = lax.axis_index("wide") == wide_size - 1
    weights = (jnp.swapaxes(diag_inverses, 1, 2), lower_blocks)
    traded = [swapped(array) for array in weights]

    received = tridiag_vectors.reshape(wide_size, subs, 128)
    received = lax.all_to_all(received, "wide", 0, 0, tiled=True)
    gram = gram_of(reflectors, 0, length // 2)
    gram, early = lax.optimization_barrier((gram, reflectors))
    v_low = early[:, last : last + half]
    received, gram, v_low = lax.optimization_barrier((received, gram, v_low))
    v_low = swapped(v_low)
    received, later = lax.optimization_barrier((received, reflectors))
    received = lax.all_to_all(received, "narrow", 0, 0, tiled=True)
    gram = gram + gram_of(later, length // 2, length)
    v_mine = jnp.where(is_owner, reflectors[:, last + half :], v_low)
    received, gram, v_mine = lax.optimization_barrier((received, gram, v_mine))
    per = wide_size // narrow_size
    received = received.reshape(narrow_size, per, subs, 128)
    flat, first, second = products_of(received, reflectors)
    z_mine = jnp.where(is_owner, flat[:, last + half :], swapped(flat[:, last : last + half]))
    first, weights, traded = lax.optimization_barrier((first, weights, traded))
    first, l_pair = summed_over_wide(first, half_pair(weights[1], traded[1], half))
    coeffs1 = dot(first, triangles[1].T)
    second = second - dot(coeffs1, gram)
    second, weights, traded = lax.optimization_barrier((second, weights, traded))
    second, d_pair = summed_over_wide(second, half_pair(weights[0], traded[0], half))
    z_mine = z_mine - dot_nt(coeffs1, v_mine[1])
    second, z_mine = lax.optimization_barrier((second, z_mine))
    coeffs0 = dot(second, triangles[0].T)
    corner = z_mine - dot_nt(coeffs0, v_mine[0])

    is_last = lax.axis_index("wide") >= wide_size - 2
    start = length - panels * panel_rows
    ends = last - panel_rows
    rows = flat.shape[0]

    def update(coeffs, first, out, unit=half):
        return updated(flat, first, coeffs, reflectors, (1, 0), first, out, unit)

    corner, late0 = lax.optimization_barrier((corner, coeffs0))
    piece2 = update([coeffs1, late0], ends, (2, 1, rows, half))
    near, remain, piece2 = from_last_chip(corner, is_last, piece2)
    near, late0 = lax.optimization_barrier((near, late0))
    rest = update([coeffs1, late0], start, (2, panels - 2, rows, half))
    remain, rest, late0 = lax.optimization_barrier((remain, rest, late0))

    def fill_first(late):
        return late, update([coeffs1, late], 0, (rows, start), 512)

    def fill_last(late):
        late, first = late
        return first, update([coeffs1, late], last, (2, 1, rows, half))

    def fill_join(late):
        first, piece3 = late
        return joined(first, [rest, piece2, piece3])

    fillers = [fill_first, fill_last, fill_join]
    transformed, solved = solve_chain(
        remain, [rest, piece2], d_pair, l_pair, is_last, late0, fillers
    )
    return (transformed, solved)


def solution(mesh):
    placed = (
        P(("wide", "narrow"), None),
        P(None, "wide", None),
        P(),
        P(None, "wide", None),
        P(None, None, "wide"),
    )
    return jax.shard_map(
        body,
        mesh=mesh,
        in_specs=placed,
        out_specs=(P("narrow", "wide"), P("narrow", None, "wide")),
        check_vma=False,
    )
```

```python
import functools

import jax
import jax.numpy as jnp
from jax import lax
from jax.experimental import pallas as pl
from jax.experimental.pallas import tpu as pltpu
from jax.sharding import PartitionSpec as P

HIGH = lax.Precision.HIGH
NN = (((1,), (0,)), ((), ()))
NT = (((1,), (1,)), ((), ()))


def dot(a, b):
    return jnp.dot(a, b, precision=HIGH)


def dot_nt(a, b):
    return lax.dot_general(a, b, NT, precision=HIGH)


def split(x):
    high = x.astype(jnp.bfloat16)
    return high, (x - high.astype(jnp.float32)).astype(jnp.bfloat16)


def dot_split(a, b, dims):
    rows = a[0].shape[0]
    both = jnp.concatenate(a, axis=0)
    with_high = lax.dot_general(both, b[0], dims, preferred_element_type=jnp.float32)
    with_low = lax.dot_general(a[0], b[1], dims, preferred_element_type=jnp.float32)
    return with_high[:rows] + (with_high[rows:] + with_low)


def in_vmem(count):
    return [pl.BlockSpec(memory_space=pltpu.VMEM)] * count


BIG = pltpu.CompilerParams(vmem_limit_bytes=50 << 20)


def held_pieces(block, which, unit, slots):
    return [
        pltpu.VMEM((slots, which, unit, block), jnp.float32),
        pltpu.SemaphoreType.DMA((slots, which)),
    ]


def dot_cost(rows, inner, outer):
    return pl.CostEstimate(
        flops=6 * rows * inner * outer,
        bytes_accessed=4 * (inner * outer + rows * inner + rows * outer),
        transcendentals=0,
    )


def pair_kernel(core_ref, own_ref, other_ref, o_ref, held, sems):
    _, pair, half = o_ref.shape
    share = pair // 2
    core = core_ref[0]
    where = pl.ds(pl.multiple_of(core * half, 128), half)
    moves = []
    for slot, (source, at) in enumerate(((own_ref, core), (other_ref, 1 - core))):
        to = o_ref.at[:, pl.ds(pl.multiple_of(at * share, 8), share), :]
        step = held.at[slot]
        moves.append(
            (
                pltpu.make_async_copy(source.at[:, :, where], step, sems.at[slot]),
                pltpu.make_async_copy(step, to, sems.at[2 + slot]),
            )
        )
    for fetch, _ in moves:
        fetch.start()
    for fetch, store in moves:
        fetch.wait()
        store.start()
    for _, store in moves:
        store.wait()


def half_pair(own, other, half):
    core = (lax.axis_index("wide") % 2)[None]
    count, share, _ = own.shape
    out = jax.ShapeDtypeStruct((count, 2 * share, half), own.dtype)
    return pl.pallas_call(
        pair_kernel,
        out_shape=out,
        in_specs=[pl.BlockSpec(memory_space=pltpu.SMEM)]
        + [pl.BlockSpec(memory_space=pl.ANY)] * 2,
        out_specs=pl.BlockSpec(memory_space=pl.ANY),
        scratch_shapes=[
            pltpu.VMEM((2, count, share, half), own.dtype),
            pltpu.SemaphoreType.DMA((4,)),
        ],
        compiler_params=pltpu.CompilerParams(vmem_limit_bytes=60 << 20),
        cost_estimate=pl.CostEstimate(
            flops=0, bytes_accessed=out.size, transcendentals=0
        ),
    )(core, own, other)


def streamed(v_ref, held, sems, which, first, count, use):
    unit = held.shape[2]
    slots = held.shape[0]

    def fetches(i):
        where = pl.ds(first + i * unit, unit)
        slot = i % slots
        return [
            pltpu.make_async_copy(
                v_ref.at[w, where, :], held.at[slot, j], sems.at[slot, j]
            )
            for j, w in enumerate(which)
        ]

    def start(i):
        for copy in fetches(i):
            copy.start()

    for i in range(min(slots, count)):
        start(i)
    for i in range(count):
        for copy in fetches(i):
            copy.wait()
        use(i, held.at[i % slots])
        if i + slots < count:
            start(i + slots)


def products_kernel(z_ref, v_ref, flat_ref, p1_ref, p0_ref, held, sems):
    unit = held.shape[2]
    _, per, subs, lanes = z_ref.shape
    sums = [jnp.zeros(p1_ref.shape, jnp.float32) for _ in range(2)]

    def use(i, v_ref):
        columns = []
        for s in range(i * unit // lanes, (i + 1) * unit // lanes):
            rows = [z_ref[:, c, s, :] for c in range(per)]
            columns.append(jnp.concatenate(rows, axis=0))
        z = jnp.concatenate(columns, axis=1)
        flat_ref[:, i * unit : (i + 1) * unit] = z
        z = split(z)
        for which in range(2):
            sums[which] = sums[which] + dot_split(z, split(v_ref[which]), NN)

    streamed(v_ref, held, sems, (0, 1), 0, subs * lanes // unit, use)
    p1_ref[...] = sums[1]
    p0_ref[...] = sums[0]


def products_of(received, reflectors):
    parts, per, subs, lanes = received.shape
    rows = parts * per
    length = subs * lanes
    block = reflectors.shape[2]
    sums = jax.ShapeDtypeStruct((rows, block), jnp.float32)
    return pl.pallas_call(
        products_kernel,
        out_shape=[jax.ShapeDtypeStruct((rows, length), jnp.float32), sums, sums],
        in_specs=in_vmem(1) + [pl.BlockSpec(memory_space=pl.ANY)],
        out_specs=in_vmem(3),
        scratch_shapes=held_pieces(block, 2, 1024, 4),
        compiler_params=BIG,
        cost_estimate=dot_cost(rows, length, 2 * block),
    )(received, reflectors)


def pieces_of(z_ref, z_first, coeffs, v_ref, held, sems, which, first, count, write):
    unit = held.shape[2]
    coeffs = [split(ref[...]) for ref in coeffs]

    def use(i, piece_ref):
        at = z_first + i * unit
        total = z_ref[:, at : at + unit]
        for j, part in enumerate(coeffs):
            total = total - dot_split(part, split(piece_ref[j]), NT)
        write(i, total)

    streamed(v_ref, held, sems, which, first, count, use)


def update_kernel(z_first, first, which, z_ref, v_ref, *refs):
    *coeffs, o_ref, held, sems = refs
    unit = held.shape[2]
    if len(o_ref.shape) == 2:
        count = o_ref.shape[1] // unit

        def write(i, total):
            o_ref[:, i * unit : (i + 1) * unit] = total

    else:
        _, panels, _, half = o_ref.shape
        each = half // unit
        count = 2 * panels * each

        def write(i, total):
            p, h, k = i // (2 * each), (i // each) % 2, i % each
            o_ref[h, p, :, k * unit : (k + 1) * unit] = total

    pieces_of(z_ref, z_first, coeffs, v_ref, held, sems, which, first, count, write)


def updated(z, z_first, coeffs, reflectors, which, first, out, unit):
    block = reflectors.shape[2]
    rows = z.shape[0]
    columns = out[1] if len(out) == 2 else 2 * out[1] * out[3]
    return pl.pallas_call(
        functools.partial(update_kernel, z_first, first, which),
        out_shape=jax.ShapeDtypeStruct(out, jnp.float32),
        in_specs=in_vmem(1) + [pl.BlockSpec(memory_space=pl.ANY)] + in_vmem(len(which)),
        out_specs=in_vmem(1)[0],
        scratch_shapes=held_pieces(block, len(which), unit, 4),
        compiler_params=BIG,
        cost_estimate=dot_cost(rows, len(which) * block, columns),
    )(z, reflectors, *coeffs)


def joined_kernel(first_ref, *refs):
    *pieces, o_ref = refs
    at = first_ref.shape[1]
    o_ref[:, :at] = first_ref[...]
    for ref in pieces:
        half = ref.shape[3]
        for q in range(ref.shape[1]):
            for h in range(2):
                o_ref[:, at : at + half] = ref[h, q]
                at += half


def joined(first, pieces):
    rows = first.shape[0]
    size = first.size + sum(x.size for x in pieces)
    return pl.pallas_call(
        joined_kernel,
        out_shape=jax.ShapeDtypeStruct((rows, size // rows), jnp.float32),
        in_specs=in_vmem(1 + len(pieces)),
        out_specs=in_vmem(1)[0],
        cost_estimate=pl.CostEstimate(
            flops=0, bytes_accessed=8 * size, transcendentals=0
        ),
    )(first, *pieces)


def swapped(array):
    size = lax.axis_size("wide")
    return lax.ppermute(array, "wide", [(i, i ^ 1) for i in range(size)])


def from_chips(array, beside=()):
    size = lax.axis_size("wide")
    array = array + lax.ppermute(array, "wide", [(i, i ^ 2) for i in range(size)])
    array, beside = lax.optimization_barrier((array, beside))
    others = [
        lax.ppermute(array, "wide", [(i, (i + by) % size) for i in range(size)])
        for by in (12, 8, 4)
    ]
    return (array + others[0]) + (others[1] + others[2]), beside


def summed_over_wide(array, beside):
    return from_chips(array + swapped(array), beside)


def from_last_chip(array, is_last, beside):
    size = lax.axis_size("wide")
    array = jnp.where(is_last, array, 0.0)
    last = size - 2
    total = array
    for back in (12, 4, 8):
        pairs = [(last + c, (last + c + back) % size) for c in range(2)]
        total = total + lax.ppermute(array, "wide", pairs)
    pairs = [(i, i ^ 2) for i in range(size) if i & 2]
    total, beside = lax.optimization_barrier((total, beside))
    return total, total + lax.ppermute(total, "wide", pairs), beside


def own_half(halves):
    is_owner = lax.axis_index("wide") == lax.axis_size("wide") - 1
    return jnp.where(is_owner, halves[1], swapped(halves[0]))


def solve_chain(remain, rest, d_pair, l_pair, is_last, late, fillers):
    panels, pair_cols, _ = d_pair.shape
    share = pair_cols // 2
    pending = []
    for piece in rest:
        owned = own_half(piece)
        pending += [jnp.where(is_last, x, 0.0) for x in owned]
    first_core = lax.axis_index("wide") % 2 == 0
    results = [None] * panels
    for source in reversed(range(panels)):
        part = dot_nt(remain, d_pair[source])
        pair = part + swapped(part)
        results[source] = jnp.where(first_core, pair[:, :share], pair[:, share:])
        offset = source * (source - 1) // 2
        for target in reversed(range(source)):
            pending[target] = pending[target] - dot(pair, l_pair[offset + target])
        if source > 0:
            urgent, late = lax.optimization_barrier((pending[source - 1], late))
            late = fillers[panels - 1 - source](late)
            remain, late = from_chips(urgent, late)
    return late, jnp.stack(results, axis=1)


def gram_of(reflectors, lo, hi):
    return lax.dot_general(
        reflectors[1, lo:hi],
        reflectors[0, lo:hi],
        (((0,), (0,)), ((), ())),
        precision=HIGH,
    )


def body(tridiag_vectors, reflectors, triangles, lower_blocks, diag_inverses):
    wide_size = lax.axis_size("wide")
    narrow_size = lax.axis_size("narrow")
    _, length, block = reflectors.shape
    panels, panel_rows, _ = diag_inverses.shape
    half = panel_rows // 2
    subs = length // 128
    last = length - panel_rows
    is_owner = lax.axis_index("wide") == wide_size - 1
    weights = (jnp.swapaxes(diag_inverses, 1, 2), lower_blocks)
    traded = [swapped(array) for array in weights]

    received = tridiag_vectors.reshape(wide_size, subs, 128)
    received = lax.all_to_all(received, "wide", 0, 0, tiled=True)
    gram = gram_of(reflectors, 0, length // 2)
    gram, early = lax.optimization_barrier((gram, reflectors))
    v_low = early[:, last : last + half]
    received, gram, v_low = lax.optimization_barrier((received, gram, v_low))
    v_low = swapped(v_low)
    received, later = lax.optimization_barrier((received, reflectors))
    received = lax.all_to_all(received, "narrow", 0, 0, tiled=True)
    gram = gram + gram_of(later, length // 2, length)
    v_mine = jnp.where(is_owner, reflectors[:, last + half :], v_low)
    received, gram, v_mine = lax.optimization_barrier((received, gram, v_mine))
    per = wide_size // narrow_size
    received = received.reshape(narrow_size, per, subs, 128)
    flat, first, second = products_of(received, reflectors)
    z_mine = jnp.where(is_owner, flat[:, last + half :], swapped(flat[:, last : last + half]))
    first, weights, traded = lax.optimization_barrier((first, weights, traded))
    first, l_pair = summed_over_wide(first, half_pair(weights[1], traded[1], half))
    coeffs1 = dot(first, triangles[1].T)
    second = second - dot(coeffs1, gram)
    second, weights, traded = lax.optimization_barrier((second, weights, traded))
    second, d_pair = summed_over_wide(second, half_pair(weights[0], traded[0], half))
    z_mine = z_mine - dot_nt(coeffs1, v_mine[1])
    second, z_mine = lax.optimization_barrier((second, z_mine))
    coeffs0 = dot(second, triangles[0].T)
    corner = z_mine - dot_nt(coeffs0, v_mine[0])

    is_last = lax.axis_index("wide") >= wide_size - 2
    start = length - panels * panel_rows
    ends = last - panel_rows
    rows = flat.shape[0]

    def update(coeffs, first, out, unit=half):
        return updated(flat, first, coeffs, reflectors, (1, 0), first, out, unit)

    corner, late0 = lax.optimization_barrier((corner, coeffs0))
    piece2 = update([coeffs1, late0], ends, (2, 1, rows, half))
    near, remain, piece2 = from_last_chip(corner, is_last, piece2)
    near, late0 = lax.optimization_barrier((near, late0))
    rest = update([coeffs1, late0], start, (2, panels - 2, rows, half))
    remain, rest, late0 = lax.optimization_barrier((remain, rest, late0))

    def fill_first(late):
        return late, update([coeffs1, late], 0, (rows, start), 512)

    def fill_last(late):
        late, first = late
        return first, update([coeffs1, late], last, (2, 1, rows, half))

    def fill_join(late):
        first, piece3 = late
        return joined(first, [rest, piece2, piece3])

    fillers = [fill_first, fill_last, fill_join]
    transformed, solved = solve_chain(
        remain, [rest, piece2], d_pair, l_pair, is_last, late0, fillers
    )
    return (transformed, solved)


def solution(mesh):
    placed = (
        P(("wide", "narrow"), None),
        P(None, "wide", None),
        P(),
        P(None, "wide", None),
        P(None, None, "wide"),
    )
    return jax.shard_map(
        body,
        mesh=mesh,
        in_specs=placed,
        out_specs=(P("narrow", "wide"), P("narrow", None, "wide")),
        check_vma=False,
    )
```

```python
import functools

import jax
import jax.numpy as jnp
from jax import lax
from jax.experimental import pallas as pl
from jax.experimental.pallas import tpu as pltpu
from jax.sharding import PartitionSpec as P

HIGH = lax.Precision.HIGH
NN = (((1,), (0,)), ((), ()))
NT = (((1,), (1,)), ((), ()))


def dot(a, b):
    return jnp.dot(a, b, precision=HIGH)


def dot_nt(a, b):
    return lax.dot_general(a, b, NT, precision=HIGH)


def split(x):
    high = x.astype(jnp.bfloat16)
    return high, (x - high.astype(jnp.float32)).astype(jnp.bfloat16)


def dot_split(a, b, dims):
    rows = a[0].shape[0]
    both = jnp.concatenate(a, axis=0)
    with_high = lax.dot_general(both, b[0], dims, preferred_element_type=jnp.float32)
    with_low = lax.dot_general(a[0], b[1], dims, preferred_element_type=jnp.float32)
    return with_high[:rows] + (with_high[rows:] + with_low)


def in_vmem(count):
    return [pl.BlockSpec(memory_space=pltpu.VMEM)] * count


BIG = pltpu.CompilerParams(vmem_limit_bytes=50 << 20)


def held_pieces(block, which, unit, slots):
    return [
        pltpu.VMEM((slots, which, unit, block), jnp.float32),
        pltpu.SemaphoreType.DMA((slots, which)),
    ]


def dot_cost(rows, inner, outer):
    return pl.CostEstimate(
        flops=6 * rows * inner * outer,
        bytes_accessed=4 * (inner * outer + rows * inner + rows * outer),
        transcendentals=0,
    )


def pair_kernel(core_ref, own_ref, other_ref, o_ref, held, sems):
    _, pair, half = o_ref.shape
    share = pair // 2
    core = core_ref[0]
    where = pl.ds(pl.multiple_of(core * half, 128), half)
    moves = []
    for slot, (source, at) in enumerate(((own_ref, core), (other_ref, 1 - core))):
        to = o_ref.at[:, pl.ds(pl.multiple_of(at * share, 8), share), :]
        step = held.at[slot]
        moves.append(
            (
                pltpu.make_async_copy(source.at[:, :, where], step, sems.at[slot]),
                pltpu.make_async_copy(step, to, sems.at[2 + slot]),
            )
        )
    for fetch, _ in moves:
        fetch.start()
    for fetch, store in moves:
        fetch.wait()
        store.start()
    for _, store in moves:
        store.wait()


def half_pair(own, other, half):
    core = (lax.axis_index("wide") % 2)[None]
    count, share, _ = own.shape
    out = jax.ShapeDtypeStruct((count, 2 * share, half), own.dtype)
    return pl.pallas_call(
        pair_kernel,
        out_shape=out,
        in_specs=[pl.BlockSpec(memory_space=pltpu.SMEM)]
        + [pl.BlockSpec(memory_space=pl.ANY)] * 2,
        out_specs=pl.BlockSpec(memory_space=pl.ANY),
        scratch_shapes=[
            pltpu.VMEM((2, count, share, half), own.dtype),
            pltpu.SemaphoreType.DMA((4,)),
        ],
        compiler_params=pltpu.CompilerParams(vmem_limit_bytes=60 << 20),
        cost_estimate=pl.CostEstimate(
            flops=0, bytes_accessed=out.size, transcendentals=0
        ),
    )(core, own, other)


def streamed(v_ref, held, sems, which, first, count, use):
    unit = held.shape[2]
    slots = held.shape[0]

    def fetches(i):
        where = pl.ds(first + i * unit, unit)
        slot = i % slots
        return [
            pltpu.make_async_copy(
                v_ref.at[w, where, :], held.at[slot, j], sems.at[slot, j]
            )
            for j, w in enumerate(which)
        ]

    def start(i):
        for copy in fetches(i):
            copy.start()

    for i in range(min(slots, count)):
        start(i)
    for i in range(count):
        for copy in fetches(i):
            copy.wait()
        use(i, held.at[i % slots])
        if i + slots < count:
            start(i + slots)


def first_products_kernel(z_ref, v_ref, flat_ref, p_ref, held, sems):
    unit = held.shape[2]
    _, per, subs, lanes = z_ref.shape
    sums = [jnp.zeros(p_ref.shape, jnp.float32)]

    def use(i, v_ref):
        columns = []
        for s in range(i * unit // lanes, (i + 1) * unit // lanes):
            rows = [z_ref[:, c, s, :] for c in range(per)]
            columns.append(jnp.concatenate(rows, axis=0))
        z = jnp.concatenate(columns, axis=1)
        flat_ref[:, i * unit : (i + 1) * unit] = z
        sums[0] = sums[0] + dot_split(split(z), split(v_ref[0]), NN)

    streamed(v_ref, held, sems, (1,), 0, subs * lanes // unit, use)
    p_ref[...] = sums[0]


def second_products_kernel(z_ref, v_ref, p_ref, held, sems):
    unit = held.shape[2]
    sums = [jnp.zeros(p_ref.shape, jnp.float32)]

    def use(i, v_ref):
        z = split(z_ref[:, i * unit : (i + 1) * unit])
        sums[0] = sums[0] + dot_split(z, split(v_ref[0]), NN)

    streamed(v_ref, held, sems, (0,), 0, z_ref.shape[1] // unit, use)
    p_ref[...] = sums[0]


def products_call(kernel, z, reflectors, outs):
    rows, block = outs[-1].shape
    return pl.pallas_call(
        kernel,
        out_shape=outs,
        in_specs=in_vmem(1) + [pl.BlockSpec(memory_space=pl.ANY)],
        out_specs=in_vmem(len(outs)),
        scratch_shapes=held_pieces(block, 1, 1024, 6),
        compiler_params=BIG,
        cost_estimate=pl.CostEstimate(
            flops=6 * z.size * block,
            bytes_accessed=z.size,
            transcendentals=0,
        ),
    )(z, reflectors)


def first_products(received, reflectors):
    parts, per, subs, lanes = received.shape
    rows = parts * per
    flat = jax.ShapeDtypeStruct((rows, subs * lanes), jnp.float32)
    sums = jax.ShapeDtypeStruct((rows, reflectors.shape[2]), jnp.float32)
    return products_call(first_products_kernel, received, reflectors, [flat, sums])


def second_products(flat, reflectors):
    sums = jax.ShapeDtypeStruct((flat.shape[0], reflectors.shape[2]), jnp.float32)
    return products_call(second_products_kernel, flat, reflectors, [sums])[0]


def pieces_of(z_ref, z_first, coeffs, v_ref, held, sems, which, first, count, write):
    unit = held.shape[2]
    coeffs = [split(ref[...]) for ref in coeffs]

    def use(i, piece_ref):
        at = z_first + i * unit
        total = z_ref[:, at : at + unit]
        for j, part in enumerate(coeffs):
            total = total - dot_split(part, split(piece_ref[j]), NT)
        write(i, total)

    streamed(v_ref, held, sems, which, first, count, use)


def update_kernel(z_first, first, which, z_ref, v_ref, *refs):
    *coeffs, o_ref, held, sems = refs
    unit = held.shape[2]
    if len(o_ref.shape) == 2:
        count = o_ref.shape[1] // unit

        def write(i, total):
            o_ref[:, i * unit : (i + 1) * unit] = total

    else:
        _, panels, _, half = o_ref.shape
        each = half // unit
        count = 2 * panels * each

        def write(i, total):
            p, h, k = i // (2 * each), (i // each) % 2, i % each
            o_ref[h, p, :, k * unit : (k + 1) * unit] = total

    pieces_of(z_ref, z_first, coeffs, v_ref, held, sems, which, first, count, write)


def updated(z, z_first, coeffs, reflectors, which, first, out, unit):
    block = reflectors.shape[2]
    rows = z.shape[0]
    columns = out[1] if len(out) == 2 else 2 * out[1] * out[3]
    return pl.pallas_call(
        functools.partial(update_kernel, z_first, first, which),
        out_shape=jax.ShapeDtypeStruct(out, jnp.float32),
        in_specs=in_vmem(1) + [pl.BlockSpec(memory_space=pl.ANY)] + in_vmem(len(which)),
        out_specs=in_vmem(1)[0],
        scratch_shapes=held_pieces(block, len(which), unit, 4),
        compiler_params=BIG,
        cost_estimate=dot_cost(rows, len(which) * block, columns),
    )(z, reflectors, *coeffs)


def joined_kernel(first_ref, *refs):
    *pieces, o_ref = refs
    at = first_ref.shape[1]
    o_ref[:, :at] = first_ref[...]
    for ref in pieces:
        half = ref.shape[3]
        for q in range(ref.shape[1]):
            for h in range(2):
                o_ref[:, at : at + half] = ref[h, q]
                at += half


def joined(first, pieces):
    rows = first.shape[0]
    size = first.size + sum(x.size for x in pieces)
    return pl.pallas_call(
        joined_kernel,
        out_shape=jax.ShapeDtypeStruct((rows, size // rows), jnp.float32),
        in_specs=in_vmem(1 + len(pieces)),
        out_specs=in_vmem(1)[0],
        cost_estimate=pl.CostEstimate(
            flops=0, bytes_accessed=8 * size, transcendentals=0
        ),
    )(first, *pieces)


def swapped(array):
    size = lax.axis_size("wide")
    return lax.ppermute(array, "wide", [(i, i ^ 1) for i in range(size)])


def from_chips(array, beside=()):
    size = lax.axis_size("wide")
    array = array + lax.ppermute(array, "wide", [(i, i ^ 2) for i in range(size)])
    array, beside = lax.optimization_barrier((array, beside))
    others = [
        lax.ppermute(array, "wide", [(i, (i + by) % size) for i in range(size)])
        for by in (12, 8, 4)
    ]
    return (array + others[0]) + (others[1] + others[2]), beside


def summed_over_wide(array, beside):
    return from_chips(array + swapped(array), beside)


def from_last_chip(array, is_last, beside):
    size = lax.axis_size("wide")
    array = jnp.where(is_last, array, 0.0)
    last = size - 2
    total = array
    for back in (12, 4, 8):
        pairs = [(last + c, (last + c + back) % size) for c in range(2)]
        total = total + lax.ppermute(array, "wide", pairs)
    pairs = [(i, i ^ 2) for i in range(size) if i & 2]
    total, beside = lax.optimization_barrier((total, beside))
    return total, total + lax.ppermute(total, "wide", pairs), beside


def own_half(halves):
    is_owner = lax.axis_index("wide") == lax.axis_size("wide") - 1
    return jnp.where(is_owner, halves[1], swapped(halves[0]))


def solve_chain(remain, rest, d_pair, l_pair, is_last, late, fillers):
    panels, pair_cols, _ = d_pair.shape
    share = pair_cols // 2
    pending = []
    for piece in rest:
        owned = own_half(piece)
        pending += [jnp.where(is_last, x, 0.0) for x in owned]
    first_core = lax.axis_index("wide") % 2 == 0
    results = [None] * panels
    for source in reversed(range(panels)):
        part = dot_nt(remain, d_pair[source])
        pair = part + swapped(part)
        results[source] = jnp.where(first_core, pair[:, :share], pair[:, share:])
        offset = source * (source - 1) // 2
        for target in reversed(range(source)):
            pending[target] = pending[target] - dot(pair, l_pair[offset + target])
        if source > 0:
            urgent, late = lax.optimization_barrier((pending[source - 1], late))
            late = fillers[panels - 1 - source](late)
            remain, late = from_chips(urgent, late)
    return late, jnp.stack(results, axis=1)


def gram_of(reflectors, lo, hi):
    return lax.dot_general(
        reflectors[1, lo:hi],
        reflectors[0, lo:hi],
        (((0,), (0,)), ((), ())),
        precision=HIGH,
    )


def body(tridiag_vectors, reflectors, triangles, lower_blocks, diag_inverses):
    wide_size = lax.axis_size("wide")
    narrow_size = lax.axis_size("narrow")
    _, length, block = reflectors.shape
    panels, panel_rows, _ = diag_inverses.shape
    half = panel_rows // 2
    subs = length // 128
    last = length - panel_rows
    is_owner = lax.axis_index("wide") == wide_size - 1
    weights = (jnp.swapaxes(diag_inverses, 1, 2), lower_blocks)
    traded = [swapped(array) for array in weights]

    received = tridiag_vectors.reshape(wide_size, subs, 128)
    received = lax.all_to_all(received, "wide", 0, 0, tiled=True)
    gram = gram_of(reflectors, 0, length // 2)
    gram, early = lax.optimization_barrier((gram, reflectors))
    v_low = early[:, last : last + half]
    received, gram, v_low = lax.optimization_barrier((received, gram, v_low))
    v_low = swapped(v_low)
    received, later = lax.optimization_barrier((received, reflectors))
    received = lax.all_to_all(received, "narrow", 0, 0, tiled=True)
    gram = gram + gram_of(later, length // 2, length)
    l_pair = half_pair(weights[1], traded[1], half)
    received, gram, l_pair = lax.optimization_barrier((received, gram, l_pair))
    per = wide_size // narrow_size
    received = received.reshape(narrow_size, per, subs, 128)
    flat, first = first_products(received, reflectors)
    z_mine = jnp.where(is_owner, flat[:, last + half :], swapped(flat[:, last : last + half]))
    first, later, v_low = lax.optimization_barrier((first, reflectors, v_low))
    first, second = summed_over_wide(first, second_products(flat, later))
    v_mine = jnp.where(is_owner, later[:, last + half :], v_low)
    first, v_mine = lax.optimization_barrier((first, v_mine))
    coeffs1 = dot(first, triangles[1].T)
    second = second - dot(coeffs1, gram)
    second, weights, traded = lax.optimization_barrier((second, weights, traded))
    second, d_pair = summed_over_wide(second, half_pair(weights[0], traded[0], half))
    z_mine = z_mine - dot_nt(coeffs1, v_mine[1])
    second, z_mine = lax.optimization_barrier((second, z_mine))
    coeffs0 = dot(second, triangles[0].T)
    corner = z_mine - dot_nt(coeffs0, v_mine[0])

    is_last = lax.axis_index("wide") >= wide_size - 2
    start = length - panels * panel_rows
    ends = last - panel_rows
    rows = flat.shape[0]

    def update(coeffs, first, out, unit=half):
        return updated(flat, first, coeffs, reflectors, (1, 0), first, out, unit)

    corner, late0 = lax.optimization_barrier((corner, coeffs0))
    piece2 = update([coeffs1, late0], ends, (2, 1, rows, half))
    near, remain, piece2 = from_last_chip(corner, is_last, piece2)
    near, late0 = lax.optimization_barrier((near, late0))
    rest = update([coeffs1, late0], start, (2, panels - 2, rows, half))
    remain, rest, late0 = lax.optimization_barrier((remain, rest, late0))

    def fill_first(late):
        return late, update([coeffs1, late], 0, (rows, start), 512)

    def fill_last(late):
        late, first = late
        return first, update([coeffs1, late], last, (2, 1, rows, half))

    def fill_join(late):
        first, piece3 = late
        return joined(first, [rest, piece2, piece3])

    fillers = [fill_first, fill_last, fill_join]
    transformed, solved = solve_chain(
        remain, [rest, piece2], d_pair, l_pair, is_last, late0, fillers
    )
    return (transformed, solved)


def solution(mesh):
    placed = (
        P(("wide", "narrow"), None),
        P(None, "wide", None),
        P(),
        P(None, "wide", None),
        P(None, None, "wide"),
    )
    return jax.shard_map(
        body,
        mesh=mesh,
        in_specs=placed,
        out_specs=(P("narrow", "wide"), P("narrow", None, "wide")),
        check_vma=False,
    )
```

```python
import functools

import jax
import jax.numpy as jnp
from jax import lax
from jax.experimental import pallas as pl
from jax.experimental.pallas import tpu as pltpu
from jax.sharding import PartitionSpec as P

HIGH = lax.Precision.HIGH
NN = (((1,), (0,)), ((), ()))
NT = (((1,), (1,)), ((), ()))


def dot(a, b):
    return jnp.dot(a, b, precision=HIGH)


def dot_nt(a, b):
    return lax.dot_general(a, b, NT, precision=HIGH)


def split(x):
    high = x.astype(jnp.bfloat16)
    return high, (x - high.astype(jnp.float32)).astype(jnp.bfloat16)


def dot_split(a, b, dims):
    rows = a[0].shape[0]
    both = jnp.concatenate(a, axis=0)
    with_high = lax.dot_general(both, b[0], dims, preferred_element_type=jnp.float32)
    with_low = lax.dot_general(a[0], b[1], dims, preferred_element_type=jnp.float32)
    return with_high[:rows] + (with_high[rows:] + with_low)


def in_vmem(count):
    return [pl.BlockSpec(memory_space=pltpu.VMEM)] * count


BIG = pltpu.CompilerParams(vmem_limit_bytes=50 << 20)


def held_pieces(block, which, unit, slots):
    return [
        pltpu.VMEM((slots, which, unit, block), jnp.float32),
        pltpu.SemaphoreType.DMA((slots, which)),
    ]


def dot_cost(rows, inner, outer):
    return pl.CostEstimate(
        flops=6 * rows * inner * outer,
        bytes_accessed=4 * (inner * outer + rows * inner + rows * outer),
        transcendentals=0,
    )


def pair_kernel(core_ref, own_ref, other_ref, o_ref, held, sems):
    _, pair, half = o_ref.shape
    share = pair // 2
    core = core_ref[0]
    where = pl.ds(pl.multiple_of(core * half, 128), half)
    moves = []
    for slot, (source, at) in enumerate(((own_ref, core), (other_ref, 1 - core))):
        to = o_ref.at[:, pl.ds(pl.multiple_of(at * share, 8), share), :]
        step = held.at[slot]
        moves.append(
            (
                pltpu.make_async_copy(source.at[:, :, where], step, sems.at[slot]),
                pltpu.make_async_copy(step, to, sems.at[2 + slot]),
            )
        )
    for fetch, _ in moves:
        fetch.start()
    for fetch, store in moves:
        fetch.wait()
        store.start()
    for _, store in moves:
        store.wait()


def half_pair(own, other, half):
    core = (lax.axis_index("wide") % 2)[None]
    count, share, _ = own.shape
    out = jax.ShapeDtypeStruct((count, 2 * share, half), own.dtype)
    return pl.pallas_call(
        pair_kernel,
        out_shape=out,
        in_specs=[pl.BlockSpec(memory_space=pltpu.SMEM)]
        + [pl.BlockSpec(memory_space=pl.ANY)] * 2,
        out_specs=pl.BlockSpec(memory_space=pl.ANY),
        scratch_shapes=[
            pltpu.VMEM((2, count, share, half), own.dtype),
            pltpu.SemaphoreType.DMA((4,)),
        ],
        compiler_params=pltpu.CompilerParams(vmem_limit_bytes=60 << 20),
        cost_estimate=pl.CostEstimate(
            flops=0, bytes_accessed=out.size, transcendentals=0
        ),
    )(core, own, other)


def streamed(v_ref, held, sems, which, first, count, use):
    unit = held.shape[2]
    slots = held.shape[0]

    def fetches(i):
        where = pl.ds(first + i * unit, unit)
        slot = i % slots
        return [
            pltpu.make_async_copy(
                v_ref.at[w, where, :], held.at[slot, j], sems.at[slot, j]
            )
            for j, w in enumerate(which)
        ]

    def start(i):
        for copy in fetches(i):
            copy.start()

    for i in range(min(slots, count)):
        start(i)
    for i in range(count):
        for copy in fetches(i):
            copy.wait()
        use(i, held.at[i % slots])
        if i + slots < count:
            start(i + slots)


def first_products_kernel(z_ref, v_ref, flat_ref, p_ref, held, sems):
    unit = held.shape[2]
    _, per, subs, lanes = z_ref.shape
    sums = [jnp.zeros(p_ref.shape, jnp.float32)]

    def use(i, v_ref):
        columns = []
        for s in range(i * unit // lanes, (i + 1) * unit // lanes):
            rows = [z_ref[:, c, s, :] for c in range(per)]
            columns.append(jnp.concatenate(rows, axis=0))
        z = jnp.concatenate(columns, axis=1)
        flat_ref[:, i * unit : (i + 1) * unit] = z
        sums[0] = sums[0] + dot_split(split(z), split(v_ref[0]), NN)

    streamed(v_ref, held, sems, (1,), 0, subs * lanes // unit, use)
    p_ref[...] = sums[0]


def second_products_kernel(z_ref, v_ref, p_ref, held, sems):
    unit = held.shape[2]
    sums = [jnp.zeros(p_ref.shape, jnp.float32)]

    def use(i, v_ref):
        z = split(z_ref[:, i * unit : (i + 1) * unit])
        sums[0] = sums[0] + dot_split(z, split(v_ref[0]), NN)

    streamed(v_ref, held, sems, (0,), 0, z_ref.shape[1] // unit, use)
    p_ref[...] = sums[0]


def products_call(kernel, z, reflectors, outs):
    rows, block = outs[-1].shape
    return pl.pallas_call(
        kernel,
        out_shape=outs,
        in_specs=in_vmem(1) + [pl.BlockSpec(memory_space=pl.ANY)],
        out_specs=in_vmem(len(outs)),
        scratch_shapes=held_pieces(block, 1, 1024, 6),
        compiler_params=BIG,
        cost_estimate=pl.CostEstimate(
            flops=6 * z.size * block,
            bytes_accessed=z.size,
            transcendentals=0,
        ),
    )(z, reflectors)


def first_products(received, reflectors):
    parts, per, subs, lanes = received.shape
    rows = parts * per
    flat = jax.ShapeDtypeStruct((rows, subs * lanes), jnp.float32)
    sums = jax.ShapeDtypeStruct((rows, reflectors.shape[2]), jnp.float32)
    return products_call(first_products_kernel, received, reflectors, [flat, sums])


def second_products(flat, reflectors):
    sums = jax.ShapeDtypeStruct((flat.shape[0], reflectors.shape[2]), jnp.float32)
    return products_call(second_products_kernel, flat, reflectors, [sums])[0]


def pieces_of(z_ref, z_first, coeffs, v_ref, held, sems, which, first, count, write):
    unit = held.shape[2]
    coeffs = [split(ref[...]) for ref in coeffs]

    def use(i, piece_ref):
        at = z_first + i * unit
        total = z_ref[:, at : at + unit]
        for j, part in enumerate(coeffs):
            total = total - dot_split(part, split(piece_ref[j]), NT)
        write(i, total)

    streamed(v_ref, held, sems, which, first, count, use)


def update_kernel(z_first, first, which, z_ref, v_ref, *refs):
    *coeffs, o_ref, held, sems = refs
    unit = held.shape[2]
    if len(o_ref.shape) == 2:
        count = o_ref.shape[1] // unit

        def write(i, total):
            o_ref[:, i * unit : (i + 1) * unit] = total

    else:
        _, panels, _, half = o_ref.shape
        each = half // unit
        count = 2 * panels * each

        def write(i, total):
            p, h, k = i // (2 * each), (i // each) % 2, i % each
            o_ref[h, p, :, k * unit : (k + 1) * unit] = total

    pieces_of(z_ref, z_first, coeffs, v_ref, held, sems, which, first, count, write)


def updated(z, z_first, coeffs, reflectors, which, first, out, unit):
    block = reflectors.shape[2]
    rows = z.shape[0]
    columns = out[1] if len(out) == 2 else 2 * out[1] * out[3]
    return pl.pallas_call(
        functools.partial(update_kernel, z_first, first, which),
        out_shape=jax.ShapeDtypeStruct(out, jnp.float32),
        in_specs=in_vmem(1) + [pl.BlockSpec(memory_space=pl.ANY)] + in_vmem(len(which)),
        out_specs=in_vmem(1)[0],
        scratch_shapes=held_pieces(block, len(which), unit, 4),
        compiler_params=BIG,
        cost_estimate=dot_cost(rows, len(which) * block, columns),
    )(z, reflectors, *coeffs)


def joined_kernel(first_ref, *refs):
    *pieces, o_ref = refs
    at = first_ref.shape[1]
    o_ref[:, :at] = first_ref[...]
    for ref in pieces:
        half = ref.shape[3]
        for q in range(ref.shape[1]):
            for h in range(2):
                o_ref[:, at : at + half] = ref[h, q]
                at += half


def joined(first, pieces):
    rows = first.shape[0]
    size = first.size + sum(x.size for x in pieces)
    return pl.pallas_call(
        joined_kernel,
        out_shape=jax.ShapeDtypeStruct((rows, size // rows), jnp.float32),
        in_specs=in_vmem(1 + len(pieces)),
        out_specs=in_vmem(1)[0],
        cost_estimate=pl.CostEstimate(
            flops=0, bytes_accessed=8 * size, transcendentals=0
        ),
    )(first, *pieces)


def swapped(array):
    size = lax.axis_size("wide")
    return lax.ppermute(array, "wide", [(i, i ^ 1) for i in range(size)])


def from_chips(array, beside=()):
    size = lax.axis_size("wide")
    array = array + lax.ppermute(array, "wide", [(i, i ^ 2) for i in range(size)])
    array, beside = lax.optimization_barrier((array, beside))
    others = [
        lax.ppermute(array, "wide", [(i, (i + by) % size) for i in range(size)])
        for by in (12, 8, 4)
    ]
    return (array + others[0]) + (others[1] + others[2]), beside


def summed_over_wide(array, beside):
    return from_chips(array + swapped(array), beside)


def from_last_chip(array, is_last, beside):
    size = lax.axis_size("wide")
    array = jnp.where(is_last, array, 0.0)
    last = size - 2
    total = array
    for back in (12, 4, 8):
        pairs = [(last + c, (last + c + back) % size) for c in range(2)]
        total = total + lax.ppermute(array, "wide", pairs)
    pairs = [(i, i ^ 2) for i in range(size) if i & 2]
    total, beside = lax.optimization_barrier((total, beside))
    return total, total + lax.ppermute(total, "wide", pairs), beside


def own_half(halves):
    is_owner = lax.axis_index("wide") == lax.axis_size("wide") - 1
    return jnp.where(is_owner, halves[1], swapped(halves[0]))


def solve_chain(remain, rest, d_pair, l_pair, is_last, late, fillers):
    panels, pair_cols, _ = d_pair.shape
    share = pair_cols // 2
    pending = []
    for piece in rest:
        owned = own_half(piece)
        pending += [jnp.where(is_last, x, 0.0) for x in owned]
    first_core = lax.axis_index("wide") % 2 == 0
    results = [None] * panels
    for source in reversed(range(panels)):
        part = dot_nt(remain, d_pair[source])
        pair = part + swapped(part)
        results[source] = jnp.where(first_core, pair[:, :share], pair[:, share:])
        offset = source * (source - 1) // 2
        for target in reversed(range(source)):
            pending[target] = pending[target] - dot(pair, l_pair[offset + target])
        if source > 0:
            urgent, late = lax.optimization_barrier((pending[source - 1], late))
            late = fillers[panels - 1 - source](late)
            remain, late = from_chips(urgent, late)
    return late, jnp.stack(results, axis=1)


def gram_of(reflectors, lo, hi):
    return lax.dot_general(
        reflectors[1, lo:hi],
        reflectors[0, lo:hi],
        (((0,), (0,)), ((), ())),
        precision=HIGH,
    )


def body(tridiag_vectors, reflectors, triangles, lower_blocks, diag_inverses):
    wide_size = lax.axis_size("wide")
    narrow_size = lax.axis_size("narrow")
    _, length, block = reflectors.shape
    panels, panel_rows, _ = diag_inverses.shape
    half = panel_rows // 2
    subs = length // 128
    last = length - panel_rows
    is_owner = lax.axis_index("wide") == wide_size - 1
    weights = (jnp.swapaxes(diag_inverses, 1, 2), lower_blocks)
    traded = [swapped(array) for array in weights]

    received = tridiag_vectors.reshape(wide_size, subs, 128)
    received = lax.all_to_all(received, "wide", 0, 0, tiled=True)
    gram = gram_of(reflectors, 0, length // 2)
    gram, early = lax.optimization_barrier((gram, reflectors))
    v_low = early[:, last : last + half]
    received, gram, v_low = lax.optimization_barrier((received, gram, v_low))
    v_low = swapped(v_low)
    received, later = lax.optimization_barrier((received, reflectors))
    received = lax.all_to_all(received, "narrow", 0, 0, tiled=True)
    gram = gram + gram_of(later, length // 2, length)
    l_pair = half_pair(weights[1], traded[1], half)
    received, gram, l_pair = lax.optimization_barrier((received, gram, l_pair))
    per = wide_size // narrow_size
    received = received.reshape(narrow_size, per, subs, 128)
    flat, first = first_products(received, reflectors)
    z_low = swapped(flat[:, last : last + half])
    first, later, v_low = lax.optimization_barrier((first, reflectors, v_low))
    first, second = summed_over_wide(first, second_products(flat, later))
    v_mine = jnp.where(is_owner, later[0, last + half :], v_low[0])
    first, v_mine = lax.optimization_barrier((first, v_mine))
    coeffs1 = dot(first, triangles[1].T)
    second = second - dot(coeffs1, gram)
    second, weights, traded = lax.optimization_barrier((second, weights, traded))
    second, d_pair = summed_over_wide(second, half_pair(weights[0], traded[0], half))
    z_mine = jnp.where(
        is_owner,
        flat[:, last + half :] - dot_nt(coeffs1, reflectors[1, last + half :]),
        z_low - dot_nt(coeffs1, v_low[1]),
    )
    second, z_mine = lax.optimization_barrier((second, z_mine))
    coeffs0 = dot(second, triangles[0].T)
    corner = z_mine - dot_nt(coeffs0, v_mine)

    is_last = lax.axis_index("wide") >= wide_size - 2
    start = length - panels * panel_rows
    ends = last - panel_rows
    rows = flat.shape[0]

    def update(coeffs, first, out, unit=half):
        return updated(flat, first, coeffs, reflectors, (1, 0), first, out, unit)

    corner, late0 = lax.optimization_barrier((corner, coeffs0))
    piece2 = update([coeffs1, late0], ends, (2, 1, rows, half))
    near, remain, piece2 = from_last_chip(corner, is_last, piece2)
    near, late0 = lax.optimization_barrier((near, late0))
    rest = update([coeffs1, late0], start, (2, panels - 2, rows, half))
    remain, rest, late0 = lax.optimization_barrier((remain, rest, late0))

    def fill_first(late):
        return late, update([coeffs1, late], 0, (rows, start), 512)

    def fill_last(late):
        late, first = late
        return first, update([coeffs1, late], last, (2, 1, rows, half))

    def fill_join(late):
        first, piece3 = late
        return joined(first, [rest, piece2, piece3])

    fillers = [fill_first, fill_last, fill_join]
    transformed, solved = solve_chain(
        remain, [rest, piece2], d_pair, l_pair, is_last, late0, fillers
    )
    return (transformed, solved)


def solution(mesh):
    placed = (
        P(("wide", "narrow"), None),
        P(None, "wide", None),
        P(),
        P(None, "wide", None),
        P(None, None, "wide"),
    )
    return jax.shard_map(
        body,
        mesh=mesh,
        in_specs=placed,
        out_specs=(P("narrow", "wide"), P("narrow", None, "wide")),
        check_vma=False,
    )
```

```python
import functools

import jax
import jax.numpy as jnp
from jax import lax
from jax.experimental import pallas as pl
from jax.experimental.pallas import tpu as pltpu
from jax.sharding import PartitionSpec as P

HIGH = lax.Precision.HIGH
NN = (((1,), (0,)), ((), ()))
NT = (((1,), (1,)), ((), ()))


def dot(a, b):
    return jnp.dot(a, b, precision=HIGH)


def dot_nt(a, b):
    return lax.dot_general(a, b, NT, precision=HIGH)


def split(x):
    high = x.astype(jnp.bfloat16)
    return high, (x - high.astype(jnp.float32)).astype(jnp.bfloat16)


def dot_split(a, b, dims):
    rows = a[0].shape[0]
    both = jnp.concatenate(a, axis=0)
    with_high = lax.dot_general(both, b[0], dims, preferred_element_type=jnp.float32)
    with_low = lax.dot_general(a[0], b[1], dims, preferred_element_type=jnp.float32)
    return with_high[:rows] + (with_high[rows:] + with_low)


def in_vmem(count):
    return [pl.BlockSpec(memory_space=pltpu.VMEM)] * count


BIG = pltpu.CompilerParams(vmem_limit_bytes=50 << 20)


def held_pieces(block, which, unit, slots):
    return [
        pltpu.VMEM((slots, which, unit, block), jnp.float32),
        pltpu.SemaphoreType.DMA((slots, which)),
    ]


def dot_cost(rows, inner, outer):
    return pl.CostEstimate(
        flops=6 * rows * inner * outer,
        bytes_accessed=4 * (inner * outer + rows * inner + rows * outer),
        transcendentals=0,
    )


def pair_kernel(core_ref, own_ref, other_ref, o_ref, held, sems):
    _, pair, half = o_ref.shape
    share = pair // 2
    core = core_ref[0]
    where = pl.ds(pl.multiple_of(core * half, 128), half)
    moves = []
    for slot, (source, at) in enumerate(((own_ref, core), (other_ref, 1 - core))):
        to = o_ref.at[:, pl.ds(pl.multiple_of(at * share, 8), share), :]
        step = held.at[slot]
        moves.append(
            (
                pltpu.make_async_copy(source.at[:, :, where], step, sems.at[slot]),
                pltpu.make_async_copy(step, to, sems.at[2 + slot]),
            )
        )
    for fetch, _ in moves:
        fetch.start()
    for fetch, store in moves:
        fetch.wait()
        store.start()
    for _, store in moves:
        store.wait()


def half_pair(own, other, half):
    core = (lax.axis_index("wide") % 2)[None]
    count, share, _ = own.shape
    out = jax.ShapeDtypeStruct((count, 2 * share, half), own.dtype)
    return pl.pallas_call(
        pair_kernel,
        out_shape=out,
        in_specs=[pl.BlockSpec(memory_space=pltpu.SMEM)]
        + [pl.BlockSpec(memory_space=pl.ANY)] * 2,
        out_specs=pl.BlockSpec(memory_space=pl.ANY),
        scratch_shapes=[
            pltpu.VMEM((2, count, share, half), own.dtype),
            pltpu.SemaphoreType.DMA((4,)),
        ],
        compiler_params=pltpu.CompilerParams(vmem_limit_bytes=60 << 20),
        cost_estimate=pl.CostEstimate(
            flops=0, bytes_accessed=out.size, transcendentals=0
        ),
    )(core, own, other)


def streamed(v_ref, held, sems, which, first, count, use):
    unit = held.shape[2]
    slots = held.shape[0]

    def fetches(i):
        where = pl.ds(first + i * unit, unit)
        slot = i % slots
        return [
            pltpu.make_async_copy(
                v_ref.at[w, where, :], held.at[slot, j], sems.at[slot, j]
            )
            for j, w in enumerate(which)
        ]

    def start(i):
        for copy in fetches(i):
            copy.start()

    for i in range(min(slots, count)):
        start(i)
    for i in range(count):
        for copy in fetches(i):
            copy.wait()
        use(i, held.at[i % slots])
        if i + slots < count:
            start(i + slots)


def first_products_kernel(z_ref, v_ref, flat_ref, p_ref, held, sems):
    unit = held.shape[2]
    _, per, subs, lanes = z_ref.shape
    sums = [jnp.zeros(p_ref.shape, jnp.float32)]

    def use(i, v_ref):
        columns = []
        for s in range(i * unit // lanes, (i + 1) * unit // lanes):
            rows = [z_ref[:, c, s, :] for c in range(per)]
            columns.append(jnp.concatenate(rows, axis=0))
        z = jnp.concatenate(columns, axis=1)
        flat_ref[:, i * unit : (i + 1) * unit] = z
        sums[0] = sums[0] + dot_split(split(z), split(v_ref[0]), NN)

    streamed(v_ref, held, sems, (1,), 0, subs * lanes // unit, use)
    p_ref[...] = sums[0]


def second_products_kernel(z_ref, v_ref, p_ref, held, sems):
    unit = held.shape[2]
    sums = [jnp.zeros(p_ref.shape, jnp.float32)]

    def use(i, v_ref):
        z = split(z_ref[:, i * unit : (i + 1) * unit])
        sums[0] = sums[0] + dot_split(z, split(v_ref[0]), NN)

    streamed(v_ref, held, sems, (0,), 0, z_ref.shape[1] // unit, use)
    p_ref[...] = sums[0]


def products_call(kernel, z, reflectors, outs):
    rows, block = outs[-1].shape
    return pl.pallas_call(
        kernel,
        out_shape=outs,
        in_specs=in_vmem(1) + [pl.BlockSpec(memory_space=pl.ANY)],
        out_specs=in_vmem(len(outs)),
        scratch_shapes=held_pieces(block, 1, 512, 8),
        compiler_params=BIG,
        cost_estimate=pl.CostEstimate(
            flops=6 * z.size * block,
            bytes_accessed=z.size,
            transcendentals=0,
        ),
    )(z, reflectors)


def first_products(received, reflectors):
    parts, per, subs, lanes = received.shape
    rows = parts * per
    flat = jax.ShapeDtypeStruct((rows, subs * lanes), jnp.float32)
    sums = jax.ShapeDtypeStruct((rows, reflectors.shape[2]), jnp.float32)
    return products_call(first_products_kernel, received, reflectors, [flat, sums])


def second_products(flat, reflectors):
    sums = jax.ShapeDtypeStruct((flat.shape[0], reflectors.shape[2]), jnp.float32)
    return products_call(second_products_kernel, flat, reflectors, [sums])[0]


def pieces_of(z_ref, z_first, coeffs, v_ref, held, sems, which, first, count, write):
    unit = held.shape[2]
    coeffs = [split(ref[...]) for ref in coeffs]

    def use(i, piece_ref):
        at = z_first + i * unit
        total = z_ref[:, at : at + unit]
        for j, part in enumerate(coeffs):
            total = total - dot_split(part, split(piece_ref[j]), NT)
        write(i, total)

    streamed(v_ref, held, sems, which, first, count, use)


def update_kernel(z_first, first, which, z_ref, v_ref, *refs):
    *coeffs, o_ref, held, sems = refs
    unit = held.shape[2]
    if len(o_ref.shape) == 2:
        count = o_ref.shape[1] // unit

        def write(i, total):
            o_ref[:, i * unit : (i + 1) * unit] = total

    else:
        _, panels, _, half = o_ref.shape
        each = half // unit
        count = 2 * panels * each

        def write(i, total):
            p, h, k = i // (2 * each), (i // each) % 2, i % each
            o_ref[h, p, :, k * unit : (k + 1) * unit] = total

    pieces_of(z_ref, z_first, coeffs, v_ref, held, sems, which, first, count, write)


def updated(z, z_first, coeffs, reflectors, which, first, out, unit):
    block = reflectors.shape[2]
    rows = z.shape[0]
    columns = out[1] if len(out) == 2 else 2 * out[1] * out[3]
    return pl.pallas_call(
        functools.partial(update_kernel, z_first, first, which),
        out_shape=jax.ShapeDtypeStruct(out, jnp.float32),
        in_specs=in_vmem(1) + [pl.BlockSpec(memory_space=pl.ANY)] + in_vmem(len(which)),
        out_specs=in_vmem(1)[0],
        scratch_shapes=held_pieces(block, len(which), unit, 4),
        compiler_params=BIG,
        cost_estimate=dot_cost(rows, len(which) * block, columns),
    )(z, reflectors, *coeffs)


def joined_kernel(first_ref, *refs):
    *pieces, o_ref = refs
    at = first_ref.shape[1]
    o_ref[:, :at] = first_ref[...]
    for ref in pieces:
        half = ref.shape[3]
        for q in range(ref.shape[1]):
            for h in range(2):
                o_ref[:, at : at + half] = ref[h, q]
                at += half


def joined(first, pieces):
    rows = first.shape[0]
    size = first.size + sum(x.size for x in pieces)
    return pl.pallas_call(
        joined_kernel,
        out_shape=jax.ShapeDtypeStruct((rows, size // rows), jnp.float32),
        in_specs=in_vmem(1 + len(pieces)),
        out_specs=in_vmem(1)[0],
        cost_estimate=pl.CostEstimate(
            flops=0, bytes_accessed=8 * size, transcendentals=0
        ),
    )(first, *pieces)


def swapped(array):
    size = lax.axis_size("wide")
    return lax.ppermute(array, "wide", [(i, i ^ 1) for i in range(size)])


def from_chips(array, beside=()):
    size = lax.axis_size("wide")
    array = array + lax.ppermute(array, "wide", [(i, i ^ 2) for i in range(size)])
    array, beside = lax.optimization_barrier((array, beside))
    others = [
        lax.ppermute(array, "wide", [(i, (i + by) % size) for i in range(size)])
        for by in (12, 8, 4)
    ]
    return (array + others[0]) + (others[1] + others[2]), beside


def summed_over_wide(array, beside):
    return from_chips(array + swapped(array), beside)


def from_last_chip(array, is_last, beside):
    size = lax.axis_size("wide")
    array = jnp.where(is_last, array, 0.0)
    last = size - 2
    total = array
    for back in (12, 4, 8):
        pairs = [(last + c, (last + c + back) % size) for c in range(2)]
        total = total + lax.ppermute(array, "wide", pairs)
    pairs = [(i, i ^ 2) for i in range(size) if i & 2]
    total, beside = lax.optimization_barrier((total, beside))
    return total, total + lax.ppermute(total, "wide", pairs), beside


def own_half(halves):
    is_owner = lax.axis_index("wide") == lax.axis_size("wide") - 1
    return jnp.where(is_owner, halves[1], swapped(halves[0]))


def solve_chain(remain, rest, d_pair, l_pair, is_last, late, fillers):
    panels, pair_cols, _ = d_pair.shape
    share = pair_cols // 2
    pending = []
    for piece in rest:
        owned = own_half(piece)
        pending += [jnp.where(is_last, x, 0.0) for x in owned]
    first_core = lax.axis_index("wide") % 2 == 0
    results = [None] * panels
    for source in reversed(range(panels)):
        part = dot_nt(remain, d_pair[source])
        pair = part + swapped(part)
        results[source] = jnp.where(first_core, pair[:, :share], pair[:, share:])
        offset = source * (source - 1) // 2
        for target in reversed(range(source)):
            pending[target] = pending[target] - dot(pair, l_pair[offset + target])
        if source > 0:
            urgent, late = lax.optimization_barrier((pending[source - 1], late))
            late = fillers[panels - 1 - source](late)
            remain, late = from_chips(urgent, late)
    return late, jnp.stack(results, axis=1)


def gram_of(reflectors, lo, hi):
    return lax.dot_general(
        reflectors[1, lo:hi],
        reflectors[0, lo:hi],
        (((0,), (0,)), ((), ())),
        precision=HIGH,
    )


def body(tridiag_vectors, reflectors, triangles, lower_blocks, diag_inverses):
    wide_size = lax.axis_size("wide")
    narrow_size = lax.axis_size("narrow")
    _, length, block = reflectors.shape
    panels, panel_rows, _ = diag_inverses.shape
    half = panel_rows // 2
    subs = length // 128
    last = length - panel_rows
    is_owner = lax.axis_index("wide") == wide_size - 1
    weights = (jnp.swapaxes(diag_inverses, 1, 2), lower_blocks)
    traded = [swapped(array) for array in weights]

    received = tridiag_vectors.reshape(wide_size, subs, 128)
    received = lax.all_to_all(received, "wide", 0, 0, tiled=True)
    gram = gram_of(reflectors, 0, length // 2)
    gram, early = lax.optimization_barrier((gram, reflectors))
    v_low = early[:, last : last + half]
    received, gram, v_low = lax.optimization_barrier((received, gram, v_low))
    v_low = swapped(v_low)
    received, later = lax.optimization_barrier((received, reflectors))
    received = lax.all_to_all(received, "narrow", 0, 0, tiled=True)
    gram = gram + gram_of(later, length // 2, length)
    l_pair = half_pair(weights[1], traded[1], half)
    received, gram, l_pair = lax.optimization_barrier((received, gram, l_pair))
    per = wide_size // narrow_size
    received = received.reshape(narrow_size, per, subs, 128)
    flat, first = first_products(received, reflectors)
    z_mine = jnp.where(is_owner, flat[:, last + half :], swapped(flat[:, last : last + half]))
    first, later, v_low = lax.optimization_barrier((first, reflectors, v_low))
    first, second = summed_over_wide(first, second_products(flat, later))
    v_mine = jnp.where(is_owner, later[:, last + half :], v_low)
    first, v_mine = lax.optimization_barrier((first, v_mine))
    coeffs1 = dot(first, triangles[1].T)
    second = second - dot(coeffs1, gram)
    second, weights, traded = lax.optimization_barrier((second, weights, traded))
    second, d_pair = summed_over_wide(second, half_pair(weights[0], traded[0], half))
    z_mine = z_mine - dot_nt(coeffs1, v_mine[1])
    second, z_mine = lax.optimization_barrier((second, z_mine))
    coeffs0 = dot(second, triangles[0].T)
    corner = z_mine - dot_nt(coeffs0, v_mine[0])

    is_last = lax.axis_index("wide") >= wide_size - 2
    start = length - panels * panel_rows
    ends = last - panel_rows
    rows = flat.shape[0]

    def update(coeffs, first, out, unit=half):
        return updated(flat, first, coeffs, reflectors, (1, 0), first, out, unit)

    corner, late0 = lax.optimization_barrier((corner, coeffs0))
    piece2 = update([coeffs1, late0], ends, (2, 1, rows, half))
    near, remain, piece2 = from_last_chip(corner, is_last, piece2)
    near, late0 = lax.optimization_barrier((near, late0))
    rest = update([coeffs1, late0], start, (2, panels - 2, rows, half))
    remain, rest, late0 = lax.optimization_barrier((remain, rest, late0))

    def fill_first(late):
        return late, update([coeffs1, late], 0, (rows, start), 512)

    def fill_last(late):
        late, first = late
        return first, update([coeffs1, late], last, (2, 1, rows, half))

    def fill_join(late):
        first, piece3 = late
        return joined(first, [rest, piece2, piece3])

    fillers = [fill_first, fill_last, fill_join]
    transformed, solved = solve_chain(
        remain, [rest, piece2], d_pair, l_pair, is_last, late0, fillers
    )
    return (transformed, solved)


def solution(mesh):
    placed = (
        P(("wide", "narrow"), None),
        P(None, "wide", None),
        P(),
        P(None, "wide", None),
        P(None, None, "wide"),
    )
    return jax.shard_map(
        body,
        mesh=mesh,
        in_specs=placed,
        out_specs=(P("narrow", "wide"), P("narrow", None, "wide")),
        check_vma=False,
    )
```
